32 devices in a mesh: seq: 8 (over y, x, core), batch: 4 (over z).
Axes of the slice: x: 2, y: 2, z: 4, core: 2. Of those that a mesh axis runs over, the one named last changes fastest.
Arguments:
- tokens: bfloat16 [4, 4096, 2048], P('batch', 'seq'), may hold values from -6 to 6
- w_qkv: bfloat16 [2048, 3072], replicated, may hold values from -0.125 to 0.125
- cotangent: bfloat16 [4, 4096, 1024], P('batch', 'seq'), may hold values from -6 to 6
Outputs:
- attended: bfloat16 [4, 4096, 1024], P('batch', 'seq')
- token_grad: bfloat16 [4, 4096, 2048], P('batch', 'seq')
- weight_grad: float32 [2048, 3072], P('seq')
The draws below stay inside these ranges and needn't reach their ends.
All inputs are finite; a program needn't handle non-finite values.
Results may differ from the reference program's by a relative error of at most 0.0064.
Values sent between devices are 32-bit elements; how exact they have to be, the bound alone decides.
A program may use at most 192 MiB of HBM per device.

```python
import jax
import jax.numpy as jnp
from jax import lax

D = 2048
HEADS = 8
DH = 128
BLK = 512
HD = 1024
SEQS = 4
LENGTH = 4096


def block_scale(rng, dims, pieces, low, high):
    level, own = 1.0, jax.random.fold_in(rng, 6)
    for dim, blocks in pieces:
        draws = jnp.exp(jax.random.uniform(jax.random.fold_in(own, dim), (blocks,), jnp.float32, low / len(pieces), high / len(pieces)))
        level = level * jnp.repeat(draws, dims[dim] // blocks).reshape([-1 if axis == dim else 1 for axis in range(len(dims))])
    return level


def bell_draw(rng, shape, spread, reach, split=(), dtype=jnp.bfloat16):
    array = spread * jax.random.normal(rng, shape, jnp.float32)
    if split:
        array = array * block_scale(rng, shape, split, -0.22, 0.18)
    return jnp.clip(array, -reach, reach).astype(dtype)


def setup_inputs(seed: int = 0) -> dict:
    keys = jax.random.split(jax.random.key(seed), 4)
    tokens = bell_draw(keys[0], (SEQS, LENGTH, D), 1.0, 6.0, ((0, 4), (1, 8)))
    w_qkv = bell_draw(keys[1], (D, 3 * HD), D ** -0.5, 0.125)
    cotangent = bell_draw(keys[2], (SEQS, LENGTH, HD), 1.0, 6.0, ((0, 4), (1, 8)))
    return dict(tokens=tokens, w_qkv=w_qkv, cotangent=cotangent)


PRECISE = lax.Precision.HIGHEST

def exclusive_running(block_states, reverse):
    zero_block = jnp.zeros_like(block_states[:1])
    if reverse:
        totals = jnp.cumsum(block_states[::-1], axis=0)[::-1]
        return jnp.concatenate([totals[1:], zero_block], 0)
    totals = jnp.cumsum(block_states, axis=0)
    return jnp.concatenate([zero_block, totals[:-1]], 0)

def rounded(value):
    low = lax.optimization_barrier(value.astype(jnp.bfloat16))
    return low.astype(jnp.float32)

def one_sequence(seq_tokens, w_qkv, seq_cotangent):
    length = seq_tokens.shape[0]
    width = w_qkv.shape[1] // 3
    block_count = length // BLK
    projected = jnp.dot(seq_tokens, w_qkv, preferred_element_type=jnp.float32).astype(jnp.bfloat16)

    def to_heads(block):
        return block.reshape(block_count, BLK, HEADS, DH).astype(jnp.float32)
    queries = to_heads(projected[:, :width])
    key_heads = to_heads(projected[:, width:2 * width])
    value_heads = to_heads(projected[:, 2 * width:])
    position = jnp.arange(length).astype(jnp.float32)
    pos_scale = DH ** (-0.5) / jnp.sqrt(position + 1.0)
    scaled_grad = (seq_cotangent.astype(jnp.float32) * pos_scale[:, None]).astype(jnp.bfloat16)
    grad_heads = to_heads(scaled_grad)
    kv_blocks = jnp.einsum('nrha,nrhb->nhab', key_heads, value_heads, precision=PRECISE)
    grad_blocks = jnp.einsum('nrha,nrhb->nhab', queries, grad_heads, precision=PRECISE)
    kv_before = exclusive_running(kv_blocks, False)
    grad_after = exclusive_running(grad_blocks, True)
    causal = jnp.arange(BLK)[:, None] >= jnp.arange(BLK)[None, :]
    scale_blocks = pos_scale.reshape(block_count, BLK)

    def one_block(block_items):
        query, key_part, value_part, grad_part, kv_state, grad_state, scale_part = block_items
        scores = rounded(jnp.where(causal, jnp.einsum('ihd,jhd->hij', query, key_part, precision=PRECISE), 0.0))
        grad_scores = rounded(jnp.where(causal, jnp.einsum('ihd,jhd->hij', grad_part, value_part, precision=PRECISE), 0.0))
        attended = jnp.einsum('hij,jhd->ihd', scores, value_part, precision=PRECISE)
        attended = (attended + jnp.einsum('ihd,hde->ihe', query, kv_state, precision=PRECISE)) * scale_part[:, None, None]
        query_grad = jnp.einsum('hij,jhd->ihd', grad_scores, key_part, precision=PRECISE)
        query_grad = query_grad + jnp.einsum('ihe,hde->ihd', grad_part, kv_state, precision=PRECISE)
        key_grad = jnp.einsum('hij,ihd->jhd', grad_scores, query, precision=PRECISE)
        key_grad = key_grad + jnp.einsum('jhe,hde->jhd', value_part, grad_state, precision=PRECISE)
        value_grad = jnp.einsum('hij,ihe->jhe', scores, grad_part, precision=PRECISE)
        value_grad = value_grad + jnp.einsum('jhd,hde->jhe', key_part, grad_state, precision=PRECISE)
        return (attended.astype(jnp.bfloat16), query_grad.astype(jnp.bfloat16), key_grad.astype(jnp.bfloat16), value_grad.astype(jnp.bfloat16))
    results = lax.map(one_block, (queries, key_heads, value_heads, grad_heads, kv_before, grad_after, scale_blocks))
    attended = results[0].reshape(length, width)
    qkv_grad = jnp.concatenate([results[1].reshape(length, width), results[2].reshape(length, width), results[3].reshape(length, width)], 1)
    token_grad = jnp.dot(qkv_grad, w_qkv.T, preferred_element_type=jnp.float32).astype(jnp.bfloat16)
    weight_part = jnp.dot(seq_tokens.T, qkv_grad, preferred_element_type=jnp.float32)
    return (attended, token_grad, weight_part)

def reference(tokens, w_qkv, cotangent):
    seq_total = tokens.shape[0]
    length = tokens.shape[1]
    attended_list = []
    token_list = []
    weight_sum = jnp.zeros(w_qkv.shape, jnp.float32)
    for number in range(seq_total):
        attended, token_grad, weight_part = one_sequence(tokens[number], w_qkv, cotangent[number])
        attended_list.append(attended)
        token_list.append(token_grad)
        weight_sum = weight_sum + weight_part
    weight_grad = weight_sum / jnp.sqrt(jnp.float32(seq_total * length))
    return (jnp.stack(attended_list, 0), jnp.stack(token_list, 0), weight_grad)
```

```python
import functools

import jax
import jax.numpy as jnp
from jax import lax
from jax.experimental import pallas as pl
from jax.experimental.pallas import tpu as pltpu
from jax.sharding import PartitionSpec as P

HEADS = 8
DH = 128
BLK = 512


PRECISE = lax.Precision.HIGHEST


def running_states(block_states, incoming, reverse):
    zero_block = jnp.zeros_like(block_states)
    if reverse:
        totals = jnp.cumsum(block_states[::-1], axis=0)[::-1]
        return incoming[None] + jnp.concatenate([totals[1:], zero_block], 0)
    totals = jnp.cumsum(block_states, axis=0)
    return incoming[None] + jnp.concatenate([zero_block, totals[:-1]], 0)


COLS = 256
MESH = pl.DeviceIdType.MESH


def bits_of(count):
    bits = count.bit_length() - 1
    assert count == 1 << bits
    return bits


def carries(kv_local, grad_local, seq_count):
    bits = bits_of(seq_count)
    rank = lax.axis_index("seq")
    half = kv_local.shape[0] // 2

    def swap(value, bit):
        return lax.ppermute(value, "seq", [(i, i ^ (1 << bit)) for i in range(seq_count)])

    def sides(value, bit):
        upper = ((rank >> bit) & 1) == 1
        return jnp.stack([jnp.where(upper, value[0], 0.0), jnp.where(upper, 0.0, value[1])])

    own = jnp.stack([kv_local, grad_local])
    other = swap(own, 0)
    near = sides(other, 0)
    total = lax.dynamic_slice_in_dim(own + other, (rank & 1) * half, half, 1)
    far = jnp.zeros_like(total)
    for bit in range(1, bits):
        other = swap(total, bit)
        far = far + sides(other, bit)
        total = total + other
    mate = swap(far, 0)
    low = (rank & 1) == 0
    joined = jnp.concatenate([jnp.where(low, far, mate), jnp.where(low, mate, far)], 1)
    result = near + joined
    return result[0], result[1]


def orders(bits):
    rest = list(range(1, bits))
    cut = len(rest) // 2
    return [[0] + rest, [0] + rest[cut:] + rest[:cut]]


def reduce_kernel(seq_count, batch_count, x_ref, g_ref, o_ref, mine, first, *rest):
    bits = bits_of(seq_count)
    lands = [first] + list(rest[: bits - 1])
    from_outer, from_inner, send_sem, recv_sem, z_send, z_recv = rest[bits - 1 :]
    chunks = mine.shape[0]
    half = mine.shape[1]
    own_rows = o_ref.shape[0]
    places = seq_count // 2
    order = orders(bits)
    rank = lax.axis_index("seq")
    plane = lax.axis_index("batch")
    middle = batch_count // 2
    low_side = plane < middle
    depth = jnp.where(low_side, middle - 1 - plane, plane - middle)
    has_outer = jnp.where(low_side, plane > 0, plane < batch_count - 1)
    is_inner = depth == 0
    inner = jnp.where(low_side, plane + 1, plane - 1)
    outer = jnp.where(low_side, plane - 1, plane + 1)

    barrier = pltpu.get_barrier_semaphore()
    for bit in range(bits):
        pl.semaphore_signal(barrier, inc=1, device_id={"seq": rank ^ (1 << bit)}, device_id_type=MESH)
    pl.semaphore_signal(barrier, inc=1, device_id={"batch": inner}, device_id_type=MESH)

    @pl.when(has_outer)
    def _():
        pl.semaphore_signal(barrier, inc=1, device_id={"batch": outer}, device_id_type=MESH)

    pl.semaphore_wait(barrier, bits + 1 + has_outer.astype(jnp.int32))

    def step_copy(chunk, step):
        size = half >> step
        source = mine.at[chunk] if step == 0 else first.at[chunk, pl.ds(size, size)]
        return pltpu.make_async_remote_copy(
            src_ref=source,
            dst_ref=lands[step].at[chunk],
            send_sem=send_sem.at[step, chunk],
            recv_sem=recv_sem.at[step, chunk],
            device_id={"seq": rank ^ (1 << order[chunk % 2][step])},
            device_id_type=MESH,
        )

    def inward(chunk, target):
        return pltpu.make_async_remote_copy(
            src_ref=first.at[chunk, pl.ds(0, own_rows)],
            dst_ref=target.at[chunk],
            send_sem=z_send.at[0, chunk],
            recv_sem=z_recv.at[0 if target is from_outer else 1, chunk],
            device_id={"batch": inner},
            device_id_type=MESH,
        )

    def outward(chunk):
        return pltpu.make_async_remote_copy(
            src_ref=from_inner.at[chunk],
            dst_ref=from_inner.at[chunk],
            send_sem=z_send.at[1, chunk],
            recv_sem=z_recv.at[1, chunk],
            device_id={"batch": outer},
            device_id_type=MESH,
        )

    def product(chunk, place):
        owner = rank ^ sum(
            (place // (1 << (bits - 1 - k)) % 2) * (1 << bit) for k, bit in enumerate(order[chunk % 2])
        )
        return jnp.dot(
            x_ref[pl.ds(pl.multiple_of(owner * own_rows, own_rows), own_rows), :],
            g_ref[:, chunk * COLS : (chunk + 1) * COLS],
            preferred_element_type=jnp.float32,
        )

    def open_chunk(chunk):
        @pl.loop(0, places)
        def _(place):
            row = pl.multiple_of(place * own_rows, own_rows)
            mine[chunk, pl.ds(row, own_rows), :] = product(chunk, places + place)

        step_copy(chunk, 0).start()

    def enter(chunk):
        step_copy(chunk, 0).wait_recv()

        @pl.loop(0, places)
        def _(place):
            row = pl.multiple_of(place * own_rows, own_rows)
            first[chunk, pl.ds(row, own_rows), :] += product(chunk, place)

        if bits > 1:
            step_copy(chunk, 1).start()

    def halve(chunk, step):
        step_copy(chunk, step).wait_recv()
        size = half >> step
        first[chunk, pl.ds(0, size), :] += lands[step][chunk]
        if step + 1 < bits:
            step_copy(chunk, step + 1).start()

    def leave(chunk):
        @pl.when(jnp.logical_not(has_outer) & jnp.logical_not(is_inner))
        def _():
            inward(chunk, from_outer).start()

        @pl.when(jnp.logical_not(has_outer) & is_inner)
        def _():
            inward(chunk, from_inner).start()

    def gather(chunk):
        @pl.when(has_outer)
        def _():
            inward(chunk, from_outer).wait_recv()
            first[chunk, pl.ds(0, own_rows), :] += from_outer[chunk]

        @pl.when(has_outer & is_inner)
        def _():
            inward(chunk, from_inner).start()

        @pl.when(has_outer & jnp.logical_not(is_inner))
        def _():
            inward(chunk, from_outer).start()

    def close(chunk):
        inward(chunk, from_inner).wait_recv()

        @pl.when(is_inner)
        def _():
            from_inner[chunk] += first[chunk, pl.ds(0, own_rows), :]

        @pl.when(has_outer)
        def _():
            outward(chunk).start()

        o_ref[:, chunk * COLS : (chunk + 1) * COLS] = from_inner[chunk]

    stages = [enter]
    stages += [functools.partial(halve, step=step) for step in range(1, bits)]
    stages += [leave, gather, close]
    lag = list(range(bits)) + [bits - 1, bits, bits + 1]
    pairs = chunks // 2
    ahead = 2
    for pair in range(min(ahead, pairs)):
        open_chunk(2 * pair)
        open_chunk(2 * pair + 1)
    for slot in range(pairs + lag[-1]):
        for stage, late in zip(stages, lag):
            pair = slot - late
            if 0 <= pair < pairs:
                stage(2 * pair)
                stage(2 * pair + 1)
            if stage is enter and slot + ahead < pairs:
                open_chunk(2 * (slot + ahead))
                open_chunk(2 * (slot + ahead) + 1)
    for chunk in range(chunks):
        for step in range(bits):
            step_copy(chunk, step).wait_send()
        inward(chunk, from_inner).wait_send()

        @pl.when(has_outer)
        def _():
            outward(chunk).wait_send()


def reduced_rows(local_x, qkv_grad, seq_count, batch_count):
    bits = bits_of(seq_count)
    positions, width = local_x.shape
    columns = qkv_grad.shape[1]
    chunks = columns // COLS
    half = width // 2
    own_rows = width // seq_count
    flops = 2 * positions * width * columns
    return pl.pallas_call(
        functools.partial(reduce_kernel, seq_count, batch_count),
        out_shape=jax.ShapeDtypeStruct((own_rows, columns), jnp.float32),
        in_specs=[pl.BlockSpec(memory_space=pltpu.VMEM)] * 2,
        out_specs=pl.BlockSpec(memory_space=pltpu.VMEM),
        scratch_shapes=[
            pltpu.VMEM((chunks, half, COLS), jnp.float32),
            pltpu.VMEM((chunks, half, COLS), jnp.float32),
            *[pltpu.VMEM((chunks, half >> step, COLS), jnp.float32) for step in range(1, bits)],
            pltpu.VMEM((chunks, own_rows, COLS), jnp.float32),
            pltpu.VMEM((chunks, own_rows, COLS), jnp.float32),
            pltpu.SemaphoreType.DMA((bits, chunks)),
            pltpu.SemaphoreType.DMA((bits, chunks)),
            pltpu.SemaphoreType.DMA((2, chunks)),
            pltpu.SemaphoreType.DMA((2, chunks)),
        ],
        compiler_params=pltpu.CompilerParams(
            collective_id=0, has_side_effects=True, vmem_limit_bytes=60 * 1024 * 1024
        ),
        cost_estimate=pl.CostEstimate(flops=flops, bytes_accessed=4 * width * columns, transcendentals=0),
    )(local_x.T, qkv_grad)


def body(tokens, w_qkv, cotangent):
    row_count = tokens.shape[1]
    width = w_qkv.shape[1] // 3
    block_count = row_count // BLK
    seq_count = lax.axis_size("seq")
    batch_count = lax.axis_size("batch")
    local_x = tokens[0]
    projected = jnp.dot(local_x, w_qkv, preferred_element_type=jnp.float32).astype(jnp.bfloat16)
    queries = projected[:, :width].reshape(block_count, BLK, HEADS, DH)
    key_heads = projected[:, width : 2 * width].reshape(block_count, BLK, HEADS, DH)
    value_heads = projected[:, 2 * width :].reshape(block_count, BLK, HEADS, DH)
    position = lax.axis_index("seq") * row_count + jnp.arange(row_count, dtype=jnp.int32)
    pos_scale = DH ** (-0.5) / jnp.sqrt(position.astype(jnp.float32) + 1.0)
    scaled_grad = (cotangent[0].astype(jnp.float32) * pos_scale[:, None]).astype(jnp.bfloat16)
    grad_heads = scaled_grad.reshape(block_count, BLK, HEADS, DH)
    kv_blocks = jnp.einsum(
        "nrha,nrhb->nhab", key_heads, value_heads, preferred_element_type=jnp.float32
    )
    grad_blocks = jnp.einsum(
        "nrha,nrhb->nhab", queries, grad_heads, preferred_element_type=jnp.float32
    )
    kv_local = jnp.sum(kv_blocks, 0)
    grad_local = jnp.sum(grad_blocks, 0)
    kv_in, grad_in = carries(kv_local, grad_local, seq_count)
    kv_before = running_states(kv_blocks, kv_in, False)
    grad_after = running_states(grad_blocks, grad_in, True)
    causal = jnp.arange(BLK)[:, None] >= jnp.arange(BLK)[None, :]
    scores = jnp.where(
        causal,
        jnp.einsum("nihd,njhd->nhij", queries, key_heads, preferred_element_type=jnp.float32),
        0.0,
    ).astype(jnp.bfloat16)
    grad_scores = jnp.where(
        causal,
        jnp.einsum("nihd,njhd->nhij", grad_heads, value_heads, preferred_element_type=jnp.float32),
        0.0,
    ).astype(jnp.bfloat16)
    query_wide = queries.astype(jnp.float32)
    key_wide = key_heads.astype(jnp.float32)
    value_wide = value_heads.astype(jnp.float32)
    grad_wide = grad_heads.astype(jnp.float32)
    attended = jnp.einsum(
        "nhij,njhd->nihd", scores, value_heads, preferred_element_type=jnp.float32
    )
    attended = attended + jnp.einsum("nihd,nhde->nihe", query_wide, kv_before, precision=PRECISE)
    attended = attended * pos_scale.reshape(block_count, BLK, 1, 1)
    query_grad = jnp.einsum(
        "nhij,njhd->nihd", grad_scores, key_heads, preferred_element_type=jnp.float32
    )
    query_grad = query_grad + jnp.einsum("nihe,nhde->nihd", grad_wide, kv_before, precision=PRECISE)
    key_grad = jnp.einsum(
        "nhij,nihd->njhd", grad_scores, queries, preferred_element_type=jnp.float32
    )
    key_grad = key_grad + jnp.einsum("njhe,nhde->njhd", value_wide, grad_after, precision=PRECISE)
    value_grad = jnp.einsum(
        "nhij,nihe->njhe", scores, grad_heads, preferred_element_type=jnp.float32
    )
    value_grad = value_grad + jnp.einsum("njhd,nhde->njhe", key_wide, grad_after, precision=PRECISE)
    qkv_grad = jnp.concatenate(
        [
            query_grad.reshape(row_count, width),
            key_grad.reshape(row_count, width),
            value_grad.reshape(row_count, width),
        ],
        1,
    ).astype(jnp.bfloat16)
    token_grad = lax.dot_general(
        qkv_grad, w_qkv, (((1,), (1,)), ((), ())), preferred_element_type=jnp.float32
    )
    token_grad = token_grad.astype(jnp.bfloat16)[None]
    summed = reduced_rows(local_x, qkv_grad, seq_count, batch_count)
    grad_scale = 1.0 / jnp.sqrt(jnp.float32(batch_count * seq_count * row_count))
    weight_grad = summed * grad_scale
    return (attended.reshape(row_count, width).astype(jnp.bfloat16)[None], token_grad, weight_grad)


def solution(mesh):
    return jax.shard_map(
        body,
        mesh=mesh,
        in_specs=(P("batch", "seq", None), P(), P("batch", "seq", None)),
        out_specs=(P("batch", "seq", None), P("batch", "seq", None), P("seq", None)),
        check_vma=False,
    )
```

```python
import functools

import jax
import jax.numpy as jnp
from jax import lax
from jax.experimental import pallas as pl
from jax.experimental.pallas import tpu as pltpu
from jax.sharding import PartitionSpec as P

HEADS = 8
DH = 128
BLK = 512


COLS = 128
MESH = pl.DeviceIdType.MESH


def bits_of(count):
    bits = count.bit_length() - 1
    assert count == 1 << bits
    return bits


def carries(own, seq_count):
    bits = bits_of(seq_count)
    rank = lax.axis_index("seq")
    half = own.shape[1] // 2

    def swap(value, bit):
        return lax.ppermute(value, "seq", [(i, i ^ (1 << bit)) for i in range(seq_count)])

    def sides(value, bit):
        upper = ((rank >> bit) & 1) == 1
        return jnp.stack([jnp.where(upper, value[0], 0.0), jnp.where(upper, 0.0, value[1])])

    other = swap(own, 0)
    near = sides(other, 0)
    total = lax.dynamic_slice_in_dim(own + other, (rank & 1) * half, half, 1)
    far = jnp.zeros_like(total)
    for bit in range(1, bits):
        other = swap(total, bit)
        far = far + sides(other, bit)
        total = total + other
    mate = swap(far, 0)
    low = (rank & 1) == 0
    joined = jnp.concatenate([jnp.where(low, far, mate), jnp.where(low, mate, far)], 1)
    result = near + joined
    return result[0], result[1]


def orders(bits):
    rest = list(range(1, bits))
    cut = len(rest) // 2
    return [[0] + rest, [0] + rest[cut:] + rest[:cut]]


def reduce_kernel(seq_count, batch_count, x_ref, g_ref, w_hbm, o_ref, t_ref, w_tiles, w_sem, mine, first, *rest):
    bits = bits_of(seq_count)
    lands = [first] + list(rest[: bits - 1])
    from_outer, from_inner, send_sem, recv_sem, z_send, z_recv = rest[bits - 1 :]
    chunks = mine.shape[0]
    half = mine.shape[1]
    own_rows = o_ref.shape[0]
    places = seq_count // 2
    order = orders(bits)
    rank = lax.axis_index("seq")
    plane = lax.axis_index("batch")
    middle = batch_count // 2
    low_side = plane < middle
    depth = jnp.where(low_side, middle - 1 - plane, plane - middle)
    has_outer = jnp.where(low_side, plane > 0, plane < batch_count - 1)
    is_inner = depth == 0
    inner = jnp.where(low_side, plane + 1, plane - 1)
    outer = jnp.where(low_side, plane - 1, plane + 1)

    barrier = pltpu.get_barrier_semaphore()
    for bit in range(bits):
        pl.semaphore_signal(barrier, inc=1, device_id={"seq": rank ^ (1 << bit)}, device_id_type=MESH)
    pl.semaphore_signal(barrier, inc=1, device_id={"batch": inner}, device_id_type=MESH)

    @pl.when(has_outer)
    def _():
        pl.semaphore_signal(barrier, inc=1, device_id={"batch": outer}, device_id_type=MESH)

    pl.semaphore_wait(barrier, bits + 1 + has_outer.astype(jnp.int32))

    def step_copy(chunk, step):
        size = half >> step
        source = mine.at[chunk] if step == 0 else first.at[chunk, pl.ds(size, size)]
        return pltpu.make_async_remote_copy(
            src_ref=source,
            dst_ref=lands[step].at[chunk],
            send_sem=send_sem.at[step, chunk],
            recv_sem=recv_sem.at[step, chunk],
            device_id={"seq": rank ^ (1 << order[chunk % 2][step])},
            device_id_type=MESH,
        )

    def inward(chunk, target):
        return pltpu.make_async_remote_copy(
            src_ref=first.at[chunk, pl.ds(0, own_rows)],
            dst_ref=target.at[chunk],
            send_sem=z_send.at[0, chunk],
            recv_sem=z_recv.at[0 if target is from_outer else 1, chunk],
            device_id={"batch": inner},
            device_id_type=MESH,
        )

    def outward(chunk):
        return pltpu.make_async_remote_copy(
            src_ref=from_inner.at[chunk],
            dst_ref=from_inner.at[chunk],
            send_sem=z_send.at[1, chunk],
            recv_sem=z_recv.at[1, chunk],
            device_id={"batch": outer},
            device_id_type=MESH,
        )

    def spots(owner_xor):
        return [
            sum((owner_xor // (1 << bit) % 2) * (1 << (bits - 1 - k)) for k, bit in enumerate(way) if k)
            for way in order
        ]

    def product(pair, owner_xor):
        owner = rank ^ owner_xor
        return jnp.dot(
            x_ref[pl.ds(pl.multiple_of(owner * own_rows, own_rows), own_rows), :],
            g_ref[:, pair * 2 * COLS : (pair + 1) * 2 * COLS],
            preferred_element_type=jnp.float32,
        )

    def open_pair(pair):
        @pl.loop(0, places)
        def _(index):
            value = product(pair, 2 * index + 1)
            for side, spot in enumerate(spots(2 * index + 1)):
                row = pl.multiple_of(spot * own_rows, own_rows)
                mine[2 * pair + side, pl.ds(row, own_rows), :] = value[:, side * COLS : (side + 1) * COLS]

        step_copy(2 * pair, 0).start()
        step_copy(2 * pair + 1, 0).start()

    def enter_pair(pair):
        step_copy(2 * pair, 0).wait_recv()
        step_copy(2 * pair + 1, 0).wait_recv()

        @pl.loop(0, places)
        def _(index):
            value = product(pair, 2 * index)
            for side, spot in enumerate(spots(2 * index)):
                row = pl.multiple_of(spot * own_rows, own_rows)
                first[2 * pair + side, pl.ds(row, own_rows), :] += value[:, side * COLS : (side + 1) * COLS]

        if bits > 1:
            step_copy(2 * pair, 1).start()
            step_copy(2 * pair + 1, 1).start()

    tile = w_tiles.shape[1]
    tiles = w_hbm.shape[0] // tile

    def w_copy(index):
        return pltpu.make_async_copy(
            w_hbm.at[pl.ds(index * tile, tile)], w_tiles.at[index % 2], w_sem.at[index % 2]
        )

    def token_tile(index):
        w_copy(index).wait()
        t_ref[:, index * tile : (index + 1) * tile] = lax.dot_general(
            g_ref[...], w_tiles[index % 2], (((1,), (1,)), ((), ())), preferred_element_type=jnp.float32
        ).astype(t_ref.dtype)
        if index + 2 < tiles:
            w_copy(index + 2).start()

    def halve(chunk, step):
        step_copy(chunk, step).wait_recv()
        size = half >> step
        first[chunk, pl.ds(0, size), :] += lands[step][chunk]
        if step + 1 < bits:
            step_copy(chunk, step + 1).start()

    def leave(chunk):
        @pl.when(jnp.logical_not(has_outer) & jnp.logical_not(is_inner))
        def _():
            inward(chunk, from_outer).start()

        @pl.when(jnp.logical_not(has_outer) & is_inner)
        def _():
            inward(chunk, from_inner).start()

    def gather(chunk):
        @pl.when(has_outer)
        def _():
            inward(chunk, from_outer).wait_recv()
            first[chunk, pl.ds(0, own_rows), :] += from_outer[chunk]

        @pl.when(has_outer & is_inner)
        def _():
            inward(chunk, from_inner).start()

        @pl.when(has_outer & jnp.logical_not(is_inner))
        def _():
            inward(chunk, from_outer).start()

    def close(chunk):
        inward(chunk, from_inner).wait_recv()

        @pl.when(is_inner)
        def _():
            from_inner[chunk] += first[chunk, pl.ds(0, own_rows), :]

        @pl.when(has_outer)
        def _():
            outward(chunk).start()

        o_ref[:, chunk * COLS : (chunk + 1) * COLS] = from_inner[chunk]

    stages = [functools.partial(halve, step=step) for step in range(1, bits)]
    stages += [leave, gather, close]
    lag = list(range(1, bits)) + [bits - 1, bits, bits + 1]
    pairs = chunks // 2
    ahead = 2
    for index in range(min(2, tiles)):
        w_copy(index).start()
    for pair in range(min(ahead, pairs)):
        open_pair(pair)
    for slot in range(pairs + lag[-1]):
        if slot < pairs:
            enter_pair(slot)
        if slot + ahead < pairs:
            open_pair(slot + ahead)
        for stage, late in zip(stages, lag):
            pair = slot - late
            if 0 <= pair < pairs:
                stage(2 * pair)
                stage(2 * pair + 1)
        if 1 <= slot <= tiles:
            token_tile(slot - 1)
    for index in range(pairs + lag[-1] - 1, tiles):
        token_tile(index)
    for chunk in range(chunks):
        for step in range(bits):
            step_copy(chunk, step).wait_send()
        inward(chunk, from_inner).wait_send()

        @pl.when(has_outer)
        def _():
            outward(chunk).wait_send()


def reduced_rows(local_x, qkv_grad, w_qkv, seq_count, batch_count):
    bits = bits_of(seq_count)
    positions, width = local_x.shape
    columns = qkv_grad.shape[1]
    chunks = columns // COLS
    half = width // 2
    own_rows = width // seq_count
    flops = 4 * positions * width * columns
    return pl.pallas_call(
        functools.partial(reduce_kernel, seq_count, batch_count),
        out_shape=(
            jax.ShapeDtypeStruct((own_rows, columns), jnp.float32),
            jax.ShapeDtypeStruct((positions, width), jnp.bfloat16),
        ),
        in_specs=[pl.BlockSpec(memory_space=pltpu.VMEM)] * 2 + [pl.BlockSpec(memory_space=pl.ANY)],
        out_specs=(pl.BlockSpec(memory_space=pltpu.VMEM), pl.BlockSpec(memory_space=pltpu.VMEM)),
        scratch_shapes=[
            pltpu.VMEM((2, 256, columns), jnp.bfloat16),
            pltpu.SemaphoreType.DMA((2,)),
            pltpu.VMEM((chunks, half, COLS), jnp.float32),
            pltpu.VMEM((chunks, half, COLS), jnp.float32),
            *[pltpu.VMEM((chunks, half >> step, COLS), jnp.float32) for step in range(1, bits)],
            pltpu.VMEM((chunks, own_rows, COLS), jnp.float32),
            pltpu.VMEM((chunks, own_rows, COLS), jnp.float32),
            pltpu.SemaphoreType.DMA((bits, chunks)),
            pltpu.SemaphoreType.DMA((bits, chunks)),
            pltpu.SemaphoreType.DMA((2, chunks)),
            pltpu.SemaphoreType.DMA((2, chunks)),
        ],
        compiler_params=pltpu.CompilerParams(
            collective_id=0, has_side_effects=True, vmem_limit_bytes=60 * 1024 * 1024
        ),
        cost_estimate=pl.CostEstimate(flops=flops, bytes_accessed=4 * width * columns, transcendentals=0),
    )(local_x.T, qkv_grad, w_qkv)


def dot(left, right, left_dim, right_dim):
    return lax.dot_general(
        left, right, (((left_dim,), (right_dim,)), ((), ())), preferred_element_type=jnp.float32
    )


def state_kernel(q_ref, k_ref, v_ref, c_ref, s_ref, g_ref, state_ref):
    grad = (c_ref[...].astype(jnp.float32) * s_ref[...]).astype(jnp.bfloat16)
    g_ref[...] = grad
    state_ref[0, 0] = dot(k_ref[...], v_ref[...], 0, 0)
    state_ref[1, 0] = dot(q_ref[...], grad, 0, 0)


def block_kernel(q_ref, k_ref, v_ref, g_ref, out_ref):
    query, key, value, grad = q_ref[...], k_ref[...], v_ref[...], g_ref[...]
    rows = lax.broadcasted_iota(jnp.int32, (BLK, BLK), 0)
    cols = lax.broadcasted_iota(jnp.int32, (BLK, BLK), 1)
    causal = rows >= cols
    scores = jnp.where(causal, dot(query, key, 1, 1), 0.0).astype(jnp.bfloat16)
    grad_scores = jnp.where(causal, dot(grad, value, 1, 1), 0.0).astype(jnp.bfloat16)
    out_ref[0] = dot(scores, value, 1, 0)
    out_ref[1] = dot(grad_scores, key, 1, 0)
    out_ref[2] = dot(grad_scores, query, 0, 0)
    out_ref[3] = dot(scores, grad, 0, 0)


def carry_kernel(q_ref, k_ref, v_ref, g_ref, s_ref, part_ref, kv_ref, gs_ref, a_ref, o_ref):
    head = pl.program_id(0)
    width = a_ref.shape[1] * pl.num_programs(0)

    def wide(left, state, state_dim):
        high = state.astype(jnp.bfloat16)
        rest = (state - high.astype(jnp.float32)).astype(jnp.bfloat16)
        return dot(left, high, 1, state_dim) + dot(left, rest, 1, state_dim)

    kv, grad_state = kv_ref[0], gs_ref[0]
    a_ref[...] = ((part_ref[0] + wide(q_ref[...], kv, 0)) * s_ref[...]).astype(a_ref.dtype)
    results = (
        part_ref[1] + wide(g_ref[...], kv, 1),
        part_ref[2] + wide(v_ref[...], grad_state, 1),
        part_ref[3] + wide(k_ref[...], grad_state, 0),
    )
    for index, result in enumerate(results):
        start = pl.multiple_of(index * width + head * DH, DH)
        o_ref[:, pl.ds(start, DH)] = result.astype(o_ref.dtype)


def body(tokens, w_qkv, cotangent):
    row_count = tokens.shape[1]
    width = w_qkv.shape[1] // 3
    assert row_count == BLK and width == HEADS * DH
    seq_count = lax.axis_size("seq")
    batch_count = lax.axis_size("batch")
    local_x = tokens[0]
    projected = jnp.dot(local_x, w_qkv, preferred_element_type=jnp.float32).astype(jnp.bfloat16)
    position = lax.axis_index("seq") * row_count + jnp.arange(row_count, dtype=jnp.int32)
    pos_scale = (DH ** (-0.5) / jnp.sqrt(position.astype(jnp.float32) + 1.0))[:, None]
    head_specs = [pl.BlockSpec((BLK, DH), lambda h, part=part: (0, part * HEADS + h)) for part in range(3)]
    own_spec = pl.BlockSpec((BLK, DH), lambda h: (0, h))
    scale_spec = pl.BlockSpec((BLK, 1), lambda h: (0, 0))
    part_spec = pl.BlockSpec((4, BLK, DH), lambda h: (0, 0, h))
    head_state = pl.BlockSpec((1, DH, DH), lambda h: (h, 0, 0))
    scaled_grad, states = pl.pallas_call(
        state_kernel,
        grid=(HEADS,),
        out_shape=(
            jax.ShapeDtypeStruct((row_count, width), jnp.bfloat16),
            jax.ShapeDtypeStruct((2, HEADS, DH, DH), jnp.float32),
        ),
        in_specs=head_specs + [own_spec, scale_spec],
        out_specs=(own_spec, pl.BlockSpec((2, 1, DH, DH), lambda h: (0, h, 0, 0))),
        cost_estimate=pl.CostEstimate(
            flops=4 * row_count * width * DH, bytes_accessed=10 * row_count * width, transcendentals=0
        ),
    )(projected, projected, projected, cotangent[0], pos_scale)
    parts = pl.pallas_call(
        block_kernel,
        grid=(HEADS,),
        out_shape=jax.ShapeDtypeStruct((4, row_count, width), jnp.float32),
        in_specs=head_specs + [own_spec],
        out_specs=part_spec,
        cost_estimate=pl.CostEstimate(
            flops=12 * row_count * width * BLK, bytes_accessed=24 * row_count * width, transcendentals=0
        ),
    )(projected, projected, projected, scaled_grad)
    kv_in, grad_in = carries(states, seq_count)
    attended, qkv_grad = pl.pallas_call(
        carry_kernel,
        grid=(HEADS,),
        out_shape=(
            jax.ShapeDtypeStruct((row_count, width), jnp.bfloat16),
            jax.ShapeDtypeStruct((row_count, 3 * width), jnp.bfloat16),
        ),
        in_specs=head_specs + [own_spec, scale_spec, part_spec, head_state, head_state],
        out_specs=(own_spec, pl.BlockSpec((BLK, 3 * width), lambda h: (0, 0))),
        cost_estimate=pl.CostEstimate(
            flops=16 * row_count * width * DH, bytes_accessed=32 * row_count * width, transcendentals=0
        ),
    )(projected, projected, projected, scaled_grad, pos_scale, parts, kv_in, grad_in)
    summed, token_grad = reduced_rows(local_x, qkv_grad, w_qkv, seq_count, batch_count)
    grad_scale = 1.0 / jnp.sqrt(jnp.float32(batch_count * seq_count * row_count))
    weight_grad = summed * grad_scale
    return attended[None], token_grad[None], weight_grad


def solution(mesh):
    return jax.shard_map(
        body,
        mesh=mesh,
        in_specs=(P("batch", "seq", None), P(), P("batch", "seq", None)),
        out_specs=(P("batch", "seq", None), P("batch", "seq", None), P("seq", None)),
        check_vma=False,
    )
```

```python
import functools

import jax
import jax.numpy as jnp
from jax import lax
from jax.experimental import pallas as pl
from jax.experimental.pallas import tpu as pltpu
from jax.sharding import PartitionSpec as P

HEADS = 8
DH = 128
BLK = 512


COLS = 128
MESH = pl.DeviceIdType.MESH


def bits_of(count):
    bits = count.bit_length() - 1
    assert count == 1 << bits
    return bits


def carries(own, seq_count, work):
    bits = bits_of(seq_count)
    rank = lax.axis_index("seq")
    half = own.shape[1] // 2

    def swap(value, bit):
        return lax.ppermute(value, "seq", [(i, i ^ (1 << bit)) for i in range(seq_count)])

    def sides(value, bit):
        upper = ((rank >> bit) & 1) == 1
        return jnp.stack([jnp.where(upper, value[0], 0.0), jnp.where(upper, 0.0, value[1])])

    other = swap(own, 0)
    near = sides(other, 0)
    total = lax.dynamic_slice_in_dim(own + other, (rank & 1) * half, half, 1)
    far = jnp.zeros_like(total)
    done = None
    for bit in range(1, bits):
        upper = ((rank >> bit) & 1) == 1
        last = bit == bits - 1
        other = swap(jnp.where(upper, total[1], total[0]) if last else total, bit)
        if bit == 1:
            done = work(total)
            other, done = lax.optimization_barrier((other, done))
        if last:
            far = far + jnp.stack([jnp.where(upper, other, 0.0), jnp.where(upper, 0.0, other)])
        else:
            far = far + sides(other, bit)
            total = total + other
    if done is None:
        done = work(total)
    mate = swap(far, 0)
    low = (rank & 1) == 0
    joined = jnp.concatenate([jnp.where(low, far, mate), jnp.where(low, mate, far)], 1)
    result = near + joined
    return result[0], result[1], done


def orders(bits):
    rest = list(range(1, bits))
    cut = len(rest) // 2
    return [[0] + rest, [0] + rest[cut:] + rest[:cut]]


def reduce_kernel(seq_count, batch_count, x_ref, g_ref, w_hbm, o_ref, t_ref, w_tiles, w_sem, mine, first, *rest):
    bits = bits_of(seq_count)
    lands = [first] + list(rest[: bits - 1])
    from_outer, from_inner, send_sem, recv_sem, z_send, z_recv = rest[bits - 1 :]
    chunks = mine.shape[0]
    half = mine.shape[1]
    own_rows = o_ref.shape[0]
    places = seq_count // 2
    order = orders(bits)
    rank = lax.axis_index("seq")
    plane = lax.axis_index("batch")
    middle = batch_count // 2
    low_side = plane < middle
    depth = jnp.where(low_side, middle - 1 - plane, plane - middle)
    has_outer = jnp.where(low_side, plane > 0, plane < batch_count - 1)
    is_inner = depth == 0
    inner = jnp.where(low_side, plane + 1, plane - 1)
    outer = jnp.where(low_side, plane - 1, plane + 1)

    barrier = pltpu.get_barrier_semaphore()
    for bit in range(bits):
        pl.semaphore_signal(barrier, inc=1, device_id={"seq": rank ^ (1 << bit)}, device_id_type=MESH)
    pl.semaphore_signal(barrier, inc=1, device_id={"batch": inner}, device_id_type=MESH)

    @pl.when(has_outer)
    def _():
        pl.semaphore_signal(barrier, inc=1, device_id={"batch": outer}, device_id_type=MESH)

    pl.semaphore_wait(barrier, bits + 1 + has_outer.astype(jnp.int32))

    def step_copy(chunk, step):
        size = half >> step
        source = mine.at[chunk] if step == 0 else first.at[chunk, pl.ds(size, size)]
        return pltpu.make_async_remote_copy(
            src_ref=source,
            dst_ref=lands[step].at[chunk],
            send_sem=send_sem.at[step, chunk],
            recv_sem=recv_sem.at[step, chunk],
            device_id={"seq": rank ^ (1 << order[chunk % 2][step])},
            device_id_type=MESH,
        )

    def inward(chunk, target):
        return pltpu.make_async_remote_copy(
            src_ref=first.at[chunk, pl.ds(0, own_rows)],
            dst_ref=target.at[chunk],
            send_sem=z_send.at[0, chunk],
            recv_sem=z_recv.at[0 if target is from_outer else 1, chunk],
            device_id={"batch": inner},
            device_id_type=MESH,
        )

    def outward(chunk):
        return pltpu.make_async_remote_copy(
            src_ref=from_inner.at[chunk],
            dst_ref=from_inner.at[chunk],
            send_sem=z_send.at[1, chunk],
            recv_sem=z_recv.at[1, chunk],
            device_id={"batch": outer},
            device_id_type=MESH,
        )

    def spots(owner_xor):
        return [
            sum((owner_xor // (1 << bit) % 2) * (1 << (bits - 1 - k)) for k, bit in enumerate(way) if k)
            for way in order
        ]

    def product(pair, owner_xor):
        owner = rank ^ owner_xor
        return jnp.dot(
            x_ref[pl.ds(pl.multiple_of(owner * own_rows, own_rows), own_rows), :],
            g_ref[:, pair * 2 * COLS : (pair + 1) * 2 * COLS],
            preferred_element_type=jnp.float32,
        )

    def open_pair(pair):
        @pl.loop(0, places)
        def _(index):
            value = product(pair, 2 * index + 1)
            for side, spot in enumerate(spots(2 * index + 1)):
                row = pl.multiple_of(spot * own_rows, own_rows)
                mine[2 * pair + side, pl.ds(row, own_rows), :] = value[:, side * COLS : (side + 1) * COLS]

        step_copy(2 * pair, 0).start()
        step_copy(2 * pair + 1, 0).start()

    def enter_pair(pair):
        step_copy(2 * pair, 0).wait_recv()
        step_copy(2 * pair + 1, 0).wait_recv()

        @pl.loop(0, places)
        def _(index):
            value = product(pair, 2 * index)
            for side, spot in enumerate(spots(2 * index)):
                row = pl.multiple_of(spot * own_rows, own_rows)
                first[2 * pair + side, pl.ds(row, own_rows), :] += value[:, side * COLS : (side + 1) * COLS]

        if bits > 1:
            step_copy(2 * pair, 1).start()
            step_copy(2 * pair + 1, 1).start()

    tile = w_tiles.shape[1]
    tiles = w_hbm.shape[0] // tile

    def w_copy(index):
        return pltpu.make_async_copy(
            w_hbm.at[pl.ds(index * tile, tile)], w_tiles.at[index % 2], w_sem.at[index % 2]
        )

    def token_tile(index):
        w_copy(index).wait()
        t_ref[:, index * tile : (index + 1) * tile] = lax.dot_general(
            g_ref[...], w_tiles[index % 2], (((1,), (1,)), ((), ())), preferred_element_type=jnp.float32
        ).astype(t_ref.dtype)
        if index + 2 < tiles:
            w_copy(index + 2).start()

    def halve(chunk, step):
        step_copy(chunk, step).wait_recv()
        size = half >> step
        first[chunk, pl.ds(0, size), :] += lands[step][chunk]
        if step + 1 < bits:
            step_copy(chunk, step + 1).start()

    def leave(chunk):
        @pl.when(jnp.logical_not(has_outer) & jnp.logical_not(is_inner))
        def _():
            inward(chunk, from_outer).start()

        @pl.when(jnp.logical_not(has_outer) & is_inner)
        def _():
            inward(chunk, from_inner).start()

    def gather(chunk):
        @pl.when(has_outer)
        def _():
            inward(chunk, from_outer).wait_recv()
            first[chunk, pl.ds(0, own_rows), :] += from_outer[chunk]

        @pl.when(has_outer & is_inner)
        def _():
            inward(chunk, from_inner).start()

        @pl.when(has_outer & jnp.logical_not(is_inner))
        def _():
            inward(chunk, from_outer).start()

    def close(chunk):
        inward(chunk, from_inner).wait_recv()

        @pl.when(is_inner)
        def _():
            from_inner[chunk] += first[chunk, pl.ds(0, own_rows), :]

        @pl.when(has_outer)
        def _():
            outward(chunk).start()

        o_ref[:, chunk * COLS : (chunk + 1) * COLS] = from_inner[chunk]

    stages = [functools.partial(halve, step=step) for step in range(1, bits)]
    stages += [leave, gather, close]
    lag = list(range(1, bits)) + [bits - 1, bits, bits + 1]
    pairs = chunks // 2
    ahead = 2
    for index in range(min(2, tiles)):
        w_copy(index).start()
    for pair in range(min(ahead, pairs)):
        open_pair(pair)
    for slot in range(pairs + lag[-1]):
        if slot < pairs:
            enter_pair(slot)
        if slot + ahead < pairs:
            open_pair(slot + ahead)
        for stage, late in zip(stages, lag):
            pair = slot - late
            if 0 <= pair < pairs:
                stage(2 * pair)
                stage(2 * pair + 1)
        if 1 <= slot <= tiles:
            token_tile(slot - 1)
    for index in range(pairs + lag[-1] - 1, tiles):
        token_tile(index)
    for chunk in range(chunks):
        for step in range(bits):
            step_copy(chunk, step).wait_send()
        inward(chunk, from_inner).wait_send()

        @pl.when(has_outer)
        def _():
            outward(chunk).wait_send()


def reduced_rows(local_x, qkv_grad, w_qkv, seq_count, batch_count):
    bits = bits_of(seq_count)
    positions, width = local_x.shape
    columns = qkv_grad.shape[1]
    chunks = columns // COLS
    half = width // 2
    own_rows = width // seq_count
    flops = 4 * positions * width * columns
    return pl.pallas_call(
        functools.partial(reduce_kernel, seq_count, batch_count),
        out_shape=(
            jax.ShapeDtypeStruct((own_rows, columns), jnp.float32),
            jax.ShapeDtypeStruct((positions, width), jnp.bfloat16),
        ),
        in_specs=[pl.BlockSpec(memory_space=pltpu.VMEM)] * 2 + [pl.BlockSpec(memory_space=pl.ANY)],
        out_specs=(pl.BlockSpec(memory_space=pltpu.VMEM), pl.BlockSpec(memory_space=pltpu.VMEM)),
        scratch_shapes=[
            pltpu.VMEM((2, 256, columns), jnp.bfloat16),
            pltpu.SemaphoreType.DMA((2,)),
            pltpu.VMEM((chunks, half, COLS), jnp.float32),
            pltpu.VMEM((chunks, half, COLS), jnp.float32),
            *[pltpu.VMEM((chunks, half >> step, COLS), jnp.float32) for step in range(1, bits)],
            pltpu.VMEM((chunks, own_rows, COLS), jnp.float32),
            pltpu.VMEM((chunks, own_rows, COLS), jnp.float32),
            pltpu.SemaphoreType.DMA((bits, chunks)),
            pltpu.SemaphoreType.DMA((bits, chunks)),
            pltpu.SemaphoreType.DMA((2, chunks)),
            pltpu.SemaphoreType.DMA((2, chunks)),
        ],
        compiler_params=pltpu.CompilerParams(
            collective_id=0, has_side_effects=True, vmem_limit_bytes=60 * 1024 * 1024
        ),
        cost_estimate=pl.CostEstimate(flops=flops, bytes_accessed=4 * width * columns, transcendentals=0),
    )(local_x.T, qkv_grad, w_qkv)


def dot(left, right, left_dim, right_dim):
    return lax.dot_general(
        left, right, (((left_dim,), (right_dim,)), ((), ())), preferred_element_type=jnp.float32
    )


def state_kernel(q_ref, k_ref, v_ref, c_ref, s_ref, g_ref, state_ref):
    grad = (c_ref[...].astype(jnp.float32) * s_ref[...]).astype(jnp.bfloat16)
    g_ref[...] = grad
    state_ref[0, 0] = dot(k_ref[...], v_ref[...], 0, 0)
    state_ref[1, 0] = dot(q_ref[...], grad, 0, 0)


def block_kernel(q_ref, k_ref, v_ref, g_ref, out_ref):
    query, key, value, grad = q_ref[...], k_ref[...], v_ref[...], g_ref[...]
    rows = lax.broadcasted_iota(jnp.int32, (BLK, BLK), 0)
    cols = lax.broadcasted_iota(jnp.int32, (BLK, BLK), 1)
    causal = rows >= cols
    scores = jnp.where(causal, dot(query, key, 1, 1), 0.0).astype(jnp.bfloat16)
    grad_scores = jnp.where(causal, dot(grad, value, 1, 1), 0.0).astype(jnp.bfloat16)
    out_ref[0] = dot(scores, value, 1, 0)
    out_ref[1] = dot(grad_scores, key, 1, 0)
    out_ref[2] = dot(grad_scores, query, 0, 0)
    out_ref[3] = dot(scores, grad, 0, 0)


def carry_kernel(q_ref, k_ref, v_ref, g_ref, s_ref, part_ref, kv_ref, gs_ref, a_ref, o_ref):
    head = pl.program_id(0)
    width = a_ref.shape[1] * pl.num_programs(0)

    def wide(left, state, state_dim):
        high = state.astype(jnp.bfloat16)
        rest = (state - high.astype(jnp.float32)).astype(jnp.bfloat16)
        return dot(left, high, 1, state_dim) + dot(left, rest, 1, state_dim)

    kv, grad_state = kv_ref[0], gs_ref[0]
    a_ref[...] = ((part_ref[0] + wide(q_ref[...], kv, 0)) * s_ref[...]).astype(a_ref.dtype)
    results = (
        part_ref[1] + wide(g_ref[...], kv, 1),
        part_ref[2] + wide(v_ref[...], grad_state, 1),
        part_ref[3] + wide(k_ref[...], grad_state, 0),
    )
    for index, result in enumerate(results):
        start = pl.multiple_of(index * width + head * DH, DH)
        o_ref[:, pl.ds(start, DH)] = result.astype(o_ref.dtype)


def body(tokens, w_qkv, cotangent):
    row_count = tokens.shape[1]
    width = w_qkv.shape[1] // 3
    assert row_count == BLK and width == HEADS * DH
    seq_count = lax.axis_size("seq")
    batch_count = lax.axis_size("batch")
    local_x = tokens[0]
    projected = jnp.dot(local_x, w_qkv, preferred_element_type=jnp.float32).astype(jnp.bfloat16)
    position = lax.axis_index("seq") * row_count + jnp.arange(row_count, dtype=jnp.int32)
    pos_scale = (DH ** (-0.5) / jnp.sqrt(position.astype(jnp.float32) + 1.0))[:, None]
    head_specs = [pl.BlockSpec((BLK, DH), lambda h, part=part: (0, part * HEADS + h)) for part in range(3)]
    own_spec = pl.BlockSpec((BLK, DH), lambda h: (0, h))
    scale_spec = pl.BlockSpec((BLK, 1), lambda h: (0, 0))
    part_spec = pl.BlockSpec((4, BLK, DH), lambda h: (0, 0, h))
    head_state = pl.BlockSpec((1, DH, DH), lambda h: (h, 0, 0))
    scaled_grad, states = pl.pallas_call(
        state_kernel,
        grid=(HEADS,),
        out_shape=(
            jax.ShapeDtypeStruct((row_count, width), jnp.bfloat16),
            jax.ShapeDtypeStruct((2, HEADS, DH, DH), jnp.float32),
        ),
        in_specs=head_specs + [own_spec, scale_spec],
        out_specs=(own_spec, pl.BlockSpec((2, 1, DH, DH), lambda h: (0, h, 0, 0))),
        cost_estimate=pl.CostEstimate(
            flops=4 * row_count * width * DH, bytes_accessed=10 * row_count * width, transcendentals=0
        ),
    )(projected, projected, projected, cotangent[0], pos_scale)
    in_block = pl.pallas_call(
        block_kernel,
        grid=(HEADS,),
        out_shape=jax.ShapeDtypeStruct((4, row_count, width), jnp.float32),
        in_specs=head_specs + [own_spec],
        out_specs=part_spec,
        cost_estimate=pl.CostEstimate(
            flops=12 * row_count * width * BLK, bytes_accessed=24 * row_count * width, transcendentals=0
        ),
    )

    def work(total):
        gated, _ = lax.optimization_barrier((scaled_grad, total))
        return in_block(projected, projected, projected, gated)

    kv_in, grad_in, parts = carries(states, seq_count, work)
    attended, qkv_grad = pl.pallas_call(
        carry_kernel,
        grid=(HEADS,),
        out_shape=(
            jax.ShapeDtypeStruct((row_count, width), jnp.bfloat16),
            jax.ShapeDtypeStruct((row_count, 3 * width), jnp.bfloat16),
        ),
        in_specs=head_specs + [own_spec, scale_spec, part_spec, head_state, head_state],
        out_specs=(own_spec, pl.BlockSpec((BLK, 3 * width), lambda h: (0, 0))),
        cost_estimate=pl.CostEstimate(
            flops=16 * row_count * width * DH, bytes_accessed=32 * row_count * width, transcendentals=0
        ),
    )(projected, projected, projected, scaled_grad, pos_scale, parts, kv_in, grad_in)
    summed, token_grad = reduced_rows(local_x, qkv_grad, w_qkv, seq_count, batch_count)
    grad_scale = 1.0 / jnp.sqrt(jnp.float32(batch_count * seq_count * row_count))
    weight_grad = summed * grad_scale
    return attended[None], token_grad[None], weight_grad


def solution(mesh):
    return jax.shard_map(
        body,
        mesh=mesh,
        in_specs=(P("batch", "seq", None), P(), P("batch", "seq", None)),
        out_specs=(P("batch", "seq", None), P("batch", "seq", None), P("seq", None)),
        check_vma=False,
    )
```
